32 devices in a mesh: row: 4 (over y, core), col: 8 (over z, x).
Axes of the slice: x: 2, y: 2, z: 4, core: 2. Of those that a mesh axis runs over, the one named last changes fastest.
Arguments:
- normal: float32 [16, 4, 256, 8, 8, 256], P(None, 'row', None, None, 'col'), may hold values from -1.5 to 1.5
- panel_inverse: float32 [256, 256], replicated, as said below
- rhs: float32 [16, 4, 256, 512], P(None, 'row', None, 'col'), may hold values from -0.009765625 to 0.009765625
- shifts: float32 [4], replicated, may hold values from 16 to 128
Outputs:
- schur: float32 [16, 4, 256, 8, 8, 256], P(None, 'row', None, None, 'col')
- eliminated: float32 [16, 4, 256, 512], P(None, 'row', None, 'col')
- applied: float32 [16, 4, 256, 512], P(None, 'row', None, 'col')
The draws below stay inside these ranges and needn't reach their ends.
Inputs may be any that keep to these rules, and one draw needn't show every extreme that they name: `panel_inverse`: lower triangular with positive diagonal entries.
All inputs are finite; a program needn't handle non-finite values.
Results may differ from the reference program's by a relative error of at most 0.000076.
Values sent between devices are 32-bit elements; how exact they have to be, the bound alone decides.
A program may use at most 256 MiB of HBM per device.

```python
import math
import jax
import jax.numpy as jnp
from jax import lax

N = 16384
NB = 256
R = 128
GROUPS = 4
BR = 16
BC = 8
K = 512
N_ROW = 4
N_COL = 8


def draw_normal(key, part):
    inner = jax.random.fold_in(key, 29)
    base = jax.random.normal(inner, (N, N), jnp.float32) * 0.25
    mirrored = (base + base.T) * 0.5 ** 0.5
    mirrored = jnp.clip(mirrored, -1.5, 1.5)
    return mirrored.reshape(BR, N_ROW, NB, BC, N_COL, NB)


def draw_panel_inverse(key, part):
    first_key, second_key = jax.random.split(jax.random.fold_in(key, 17))
    diagonal = jax.random.uniform(first_key, (NB,), jnp.float32, 0.5, 1.5)
    offdiag = jax.random.normal(second_key, (NB, NB), jnp.float32) * (0.5 / NB ** 0.5)
    return jnp.tril(offdiag, -1) + jnp.diag(diagonal)


def steps_of(rng, dims, cuts, smallest, high):
    factor_of = 1.0
    for dim, parts in cuts:
        draws = jax.random.uniform(jax.random.fold_in(jax.random.fold_in(rng, 6), dim), (parts,), jnp.float32, smallest / len(cuts), high / len(cuts))
        factor_of = factor_of * jnp.repeat(jnp.exp(draws), dims[dim] // parts).reshape((-1,) + (1,) * (len(dims) - 1 - dim))
    return factor_of


def noise(own_key, shape, width, limit, cuts=(), held_as=jnp.bfloat16):
    result = jax.random.normal(own_key, shape, jnp.float32) * width
    if len(cuts) > 0:
        result = steps_of(own_key, shape, cuts, -0.22, 0.18) * result
    return jnp.clip(result, min=-limit, max=limit).astype(held_as)


def setup_inputs(seed: int = 0) -> dict:
    streams_of = jax.random.split(jax.random.key(seed), 5)
    normal = draw_normal(jax.random.fold_in(streams_of[4], 71), 0)
    panel_inverse = draw_panel_inverse(jax.random.fold_in(streams_of[4], 71), 0)
    rhs = noise(streams_of[2], (BR, N_ROW, NB, K), 0.0016, 0.009765625, ((1, 4), (3, 8)), jnp.float32)
    shifts = jnp.clip(jnp.exp(jax.random.uniform(streams_of[3], (GROUPS,), jnp.float32, math.log(16.0), math.log(128.0))), 16.0, 128.0)
    return dict(normal=normal, panel_inverse=panel_inverse, rhs=rhs, shifts=shifts)


def reference(normal, panel_inverse, rhs, shifts):
    high = lax.Precision.HIGHEST
    matrix = normal.reshape(N, N)
    right = rhs.reshape(N, K)
    panel = jnp.dot(matrix[:, :NB], panel_inverse.T, precision=high, preferred_element_type=jnp.float32)
    updated = matrix - jnp.dot(panel, panel.T, precision=high, preferred_element_type=jnp.float32)
    first = jnp.dot(panel_inverse, right[:NB], precision=high, preferred_element_type=jnp.float32)
    reduced = right - jnp.dot(panel, first, precision=high, preferred_element_type=jnp.float32)
    reduced = jnp.concatenate([first, reduced[NB:]], axis=0)
    scales = jnp.repeat(shifts, R)
    product = jnp.dot(updated, reduced, precision=high, preferred_element_type=jnp.float32) + reduced * scales[None, :]
    schur = updated.reshape(BR, N_ROW, NB, BC, N_COL, NB)
    return schur, reduced.reshape(BR, N_ROW, NB, K), product.reshape(BR, N_ROW, NB, K)
```

```python
import functools

import jax
import jax.numpy as jnp
from jax import lax
from jax.experimental import pallas as pl
from jax.experimental.pallas import tpu as pltpu
from jax.sharding import PartitionSpec as P

R = 128
LANES = 128
F32 = jnp.float32
BF16 = jnp.bfloat16


def split(value):
    high = value.astype(BF16)
    low = (value - high.astype(F32)).astype(BF16)
    return high, low


def left_of(value):
    high, low = split(value)
    return jnp.concatenate([high, high, low], axis=1)


def right_of(value):
    high, low = split(value)
    return jnp.concatenate([high, low, high], axis=0)


def dot(left, right):
    return jnp.dot(left, right, preferred_element_type=F32)


def fused_kernel(bcols, nb, narrow, tile_ref, panel_ref, across_ref, rhs_ref, first_ref,
                 schur_ref, own_ref, total_ref, across3, first3, reduced):
    step = pl.program_id(0)
    stride = bcols * nb // LANES
    per = nb // LANES
    wide = first_ref.shape[0]

    @pl.when(step == 0)
    def _():
        across3[...] = right_of(across_ref[...])
        first3[...] = left_of(first_ref[...])
        total_ref[...] = jnp.zeros_like(total_ref)

    panel = panel_ref[...]
    panel3 = left_of(panel)
    high, low = split(panel)
    flat3 = jnp.concatenate([high, low, high], axis=1)
    lowered = lax.dot_general(
        first3[...], flat3, (((1,), (1,)), ((), ())), preferred_element_type=F32
    )
    value = rhs_ref[...].reshape(wide, nb) - lowered
    leading = jnp.logical_and(step == 0, lax.axis_index("row") == 0)
    value = jnp.where(leading, first_ref[...], value)
    reduced[...] = value
    mine = pl.multiple_of(lax.axis_index("col") * narrow, narrow)
    own_ref[0] = reduced[pl.ds(mine, narrow), :]
    value3 = left_of(value)
    for b in range(bcols):
        columns = slice(b * nb, (b + 1) * nb)
        product = dot(panel3, across3[:, columns])
        parts = []
        for h in range(per):
            rows = pl.ds(b * per + h, nb, stride=stride)
            part = tile_ref[rows, :] - product[:, h * LANES:(h + 1) * LANES]
            schur_ref[rows, :] = part
            parts.append(part)
        updated = jnp.concatenate(parts, axis=1)
        total_ref[:, columns] += dot(value3, right_of(updated))


def fused(tile, panel, across, gathered, first, brows, bcols, nb, narrow):
    wide = first.shape[0]
    ncol = wide // narrow
    chunk = nb * bcols * nb // LANES
    whole = lambda i: (0, 0)
    return pl.pallas_call(
        functools.partial(fused_kernel, bcols, nb, narrow),
        grid=(brows,),
        in_specs=[
            pl.BlockSpec((chunk, LANES), lambda i: (i, 0)),
            pl.BlockSpec((nb, nb), lambda i: (i, 0)),
            pl.BlockSpec((nb, bcols * nb), whole),
            pl.BlockSpec((ncol, None, narrow, nb), lambda i: (0, i, 0, 0)),
            pl.BlockSpec((wide, nb), whole),
        ],
        out_specs=[
            pl.BlockSpec((chunk, LANES), lambda i: (i, 0)),
            pl.BlockSpec((1, narrow, nb), lambda i: (i, 0, 0)),
            pl.BlockSpec((wide, bcols * nb), whole),
        ],
        out_shape=[
            jax.ShapeDtypeStruct(tile.shape, F32),
            jax.ShapeDtypeStruct((brows, narrow, nb), F32),
            jax.ShapeDtypeStruct((wide, bcols * nb), F32),
        ],
        scratch_shapes=[
            pltpu.VMEM((3 * nb, bcols * nb), BF16),
            pltpu.VMEM((wide, 3 * nb), BF16),
            pltpu.VMEM((wide, nb), F32),
        ],
        compiler_params=pltpu.CompilerParams(
            dimension_semantics=("arbitrary",), vmem_limit_bytes=48 * 2**20
        ),
    )(tile, panel, across, gathered, first)


def spread(value, axis, source):
    return lax.psum(jnp.where(lax.axis_index(axis) == source, value, 0.0), axis)


def shards(normal, panel_inverse, rhs, shifts):
    high = lax.Precision.HIGHEST
    row_index = lax.axis_index("row")
    col_index = lax.axis_index("col")
    nrow = lax.axis_size("row")
    ncol = lax.axis_size("col")
    spacing = ncol // nrow
    brows, nb, bcols = (normal.shape[0], normal.shape[2], normal.shape[3])
    narrow = rhs.shape[3]
    wide = narrow * ncol
    right = jnp.transpose(rhs[:, 0], (0, 2, 1))
    across = spread(normal[0, 0].reshape(nb, bcols * nb), "row", 0)
    leading = spread(right[0], "row", 0)
    gathered = lax.all_gather(jnp.concatenate([right, leading[None]], axis=0), "col", axis=0)
    column = spread(normal[:, 0, :, 0, 0, :].reshape(brows * nb, nb), "col", 0)
    panel = jnp.dot(column, panel_inverse.T, precision=high, preferred_element_type=F32)
    across = jnp.dot(panel_inverse, across, precision=high, preferred_element_type=F32)
    first = jnp.dot(
        gathered[:, brows].reshape(wide, nb), panel_inverse.T, precision=high,
        preferred_element_type=F32,
    )
    tile = normal.reshape(brows * nb * bcols * nb // LANES, LANES)
    schur, reduced, total = fused(
        tile, panel, across, gathered, first, brows, bcols, nb, narrow
    )
    part = lax.psum_scatter(total, "row", scatter_dimension=0, tiled=True)
    part = part.reshape(spacing, narrow, bcols * nb)
    offset = col_index // nrow
    arrived = []
    for t in range(spacing):
        moves = [
            (p * ncol + q, (q % nrow) * ncol + spacing * p + (q // nrow + t) % spacing)
            for p in range(nrow)
            for q in range(ncol)
        ]
        piece = lax.dynamic_index_in_dim(part, (offset + t) % spacing, 0, keepdims=False)
        arrived.append(lax.ppermute(piece, ("row", "col"), moves))
    arrived = jnp.stack(arrived)
    place = col_index % spacing
    ordered = [
        lax.dynamic_index_in_dim(arrived, (place - o + spacing) % spacing, 0, keepdims=False)
        for o in range(spacing)
    ]
    product = jnp.stack([o.reshape(narrow, bcols, nb) for o in ordered])
    product = jnp.transpose(product, (2, 0, 1, 3)).reshape(brows, narrow, nb)
    scales = lax.dynamic_slice_in_dim(jnp.repeat(shifts, R), col_index * narrow, narrow)
    applied = product + reduced * scales[None, :, None]
    back = lambda value: jnp.transpose(value, (0, 2, 1)).reshape(brows, 1, nb, narrow)
    return (schur.reshape(normal.shape), back(reduced), back(applied))


def solution(mesh):
    in_specs = (P(None, "row", None, None, "col", None), P(), P(None, "row", None, "col"), P())
    out_specs = (
        P(None, "row", None, None, "col", None),
        P(None, "row", None, "col"),
        P(None, "row", None, "col"),
    )
    return jax.shard_map(shards, mesh=mesh, in_specs=in_specs, out_specs=out_specs, check_vma=False)
```

```python
import functools

import jax
import jax.numpy as jnp
from jax import lax
from jax.experimental import pallas as pl
from jax.experimental.pallas import tpu as pltpu
from jax.sharding import PartitionSpec as P

R = 128
LANES = 128
F32 = jnp.float32
BF16 = jnp.bfloat16


def split(value):
    high = value.astype(BF16)
    low = (value - high.astype(F32)).astype(BF16)
    return high, low


def left_of(value):
    high, low = split(value)
    return jnp.concatenate([high, high, low], axis=1)


def right_of(value):
    high, low = split(value)
    return jnp.concatenate([high, low, high], axis=0)


def dot(left, right):
    return jnp.dot(left, right, preferred_element_type=F32)


def fused_kernel(bcols, nb, narrow, tile_ref, panel_ref, across_ref, rhs_ref, first_ref,
                 schur_ref, own_ref, total_ref, across3, first3, reduced):
    step = pl.program_id(0)
    stride = bcols * nb // LANES
    per = nb // LANES
    wide = first_ref.shape[0]

    @pl.when(step == 0)
    def _():
        across3[...] = right_of(across_ref[...])
        first3[...] = left_of(first_ref[...])
        total_ref[...] = jnp.zeros_like(total_ref)

    panel = panel_ref[...]
    panel3 = left_of(panel)
    high, low = split(panel)
    flat3 = jnp.concatenate([high, low, high], axis=1)
    lowered = lax.dot_general(
        first3[...], flat3, (((1,), (1,)), ((), ())), preferred_element_type=F32
    )
    value = rhs_ref[...].reshape(wide, nb) - lowered
    leading = jnp.logical_and(step == 0, lax.axis_index("row") == 0)
    value = jnp.where(leading, first_ref[...], value)
    reduced[...] = value
    mine = pl.multiple_of(lax.axis_index("col") * narrow, narrow)
    own_ref[0] = reduced[pl.ds(mine, narrow), :]
    value3 = left_of(value)
    for b in range(bcols):
        columns = slice(b * nb, (b + 1) * nb)
        product = dot(panel3, across3[:, columns])
        parts = []
        for h in range(per):
            rows = pl.ds(b * per + h, nb, stride=stride)
            part = tile_ref[rows, :] - product[:, h * LANES:(h + 1) * LANES]
            schur_ref[rows, :] = part
            parts.append(part)
        updated = jnp.concatenate(parts, axis=1)
        total_ref[:, columns] += dot(value3, right_of(updated))


def fused(tile, panel, across, gathered, first, brows, bcols, nb, narrow):
    wide = first.shape[0]
    ncol = wide // narrow
    chunk = nb * bcols * nb // LANES
    whole = lambda i: (0, 0)
    return pl.pallas_call(
        functools.partial(fused_kernel, bcols, nb, narrow),
        grid=(brows,),
        in_specs=[
            pl.BlockSpec((chunk, LANES), lambda i: (i, 0)),
            pl.BlockSpec((nb, nb), lambda i: (i, 0)),
            pl.BlockSpec((nb, bcols * nb), whole),
            pl.BlockSpec((ncol, None, narrow, nb), lambda i: (0, i, 0, 0)),
            pl.BlockSpec((wide, nb), whole),
        ],
        out_specs=[
            pl.BlockSpec((chunk, LANES), lambda i: (i, 0)),
            pl.BlockSpec((1, narrow, nb), lambda i: (i, 0, 0)),
            pl.BlockSpec((wide, bcols * nb), whole),
        ],
        out_shape=[
            jax.ShapeDtypeStruct(tile.shape, F32),
            jax.ShapeDtypeStruct((brows, narrow, nb), F32),
            jax.ShapeDtypeStruct((wide, bcols * nb), F32),
        ],
        scratch_shapes=[
            pltpu.VMEM((3 * nb, bcols * nb), BF16),
            pltpu.VMEM((wide, 3 * nb), BF16),
            pltpu.VMEM((wide, nb), F32),
        ],
        compiler_params=pltpu.CompilerParams(
            dimension_semantics=("arbitrary",), vmem_limit_bytes=48 * 2**20
        ),
    )(tile, panel, across, gathered, first)


def spread_kernel(ncol, nrow, chunks, column_in, block_in, lead_in,
                  column_out, block_out, lead_out,
                  column_send, column_recv, block_send, block_recv,
                  lead_send, lead_recv, peer_send, peer_recv, local):
    p = lax.axis_index("row")
    q = lax.axis_index("col")
    barrier = pltpu.get_barrier_semaphore()
    for d in range(1, ncol):
        pl.semaphore_signal(barrier, inc=1, device_id={"col": (q + d) % ncol})
    for d in range(1, nrow):
        pl.semaphore_signal(barrier, inc=1, device_id={"row": (p + d) % nrow})
    pl.semaphore_wait(barrier, ncol + nrow - 2)

    targets = [(p + 1, jnp.logical_and(p % 2 == 0, p + 1 < nrow)),
               (p + 2, jnp.logical_and(p % 2 == 0, p + 2 < nrow))]

    def lead_copy(source, way):
        return pltpu.make_async_remote_copy(
            source, lead_out.at[q], lead_send.at[way], lead_recv,
            device_id={"row": targets[way][0] % nrow})

    def peer_copy(source, d):
        return pltpu.make_async_remote_copy(
            source, lead_out.at[q], peer_send.at[d], peer_recv.at[d],
            device_id={"col": (q + d) % ncol})

    def lead_onward(source):
        for way in range(2):
            @pl.when(targets[way][1])
            def _(way=way):
                lead_copy(source, way).start()
        for d in range(1, ncol):
            peer_copy(source, d).start()

    @pl.when(p == 0)
    def _():
        pltpu.make_async_copy(lead_in, lead_out.at[q], local).start()
        lead_onward(lead_in)
        pltpu.make_async_copy(lead_in, lead_out.at[q], local).wait()

    @pl.when(p > 0)
    def _():
        lead_copy(lead_in, 0).wait_recv()
        lead_onward(lead_out.at[q])

    odd = q % 2
    place = (1 - odd) * (q // 2) + odd * (ncol - 1 - q // 2)

    def at_place(k):
        k = k % ncol
        late = k // (ncol // 2)
        return (1 - late) * 2 * k + late * (2 * (ncol - 1 - k) + 1)

    ways = [(place, at_place(place + 1)), ((ncol - place) % ncol, at_place(place + ncol - 1))]
    size = column_in.shape[0] // (2 * chunks)
    thin = block_in.shape[0] // chunks

    def column_copy(source, way, c):
        rows = pl.ds(pl.multiple_of((way * chunks + c) * size, size), size)
        return pltpu.make_async_remote_copy(
            source.at[rows], column_out.at[rows], column_send.at[way, c],
            column_recv.at[way, c], device_id={"col": ways[way][1]})

    def block_copy(source, way, c):
        rows = pl.ds(pl.multiple_of(c * thin, thin), thin)
        return pltpu.make_async_remote_copy(
            source.at[rows], block_out.at[rows], block_send.at[way, c],
            block_recv.at[c], device_id={"row": targets[way][0] % nrow})

    def block_onward(source, c):
        for way in range(2):
            @pl.when(targets[way][1])
            def _(way=way):
                block_copy(source, way, c).start()

    deep = p // 2 + p % 2

    @pl.loop(0, chunks + ncol + nrow)
    def _(step):
        for way in range(2):
            depth = ways[way][0]
            c = step - depth

            @pl.when(jnp.logical_and(c >= 0, c < chunks))
            def _(way=way, depth=depth, c=c):
                @pl.when(depth == 0)
                def _():
                    column_copy(column_in, way, c).start()

                @pl.when(depth > 0)
                def _():
                    column_copy(column_in, way, c).wait_recv()

                    @pl.when(depth < ncol - 1)
                    def _():
                        column_copy(column_out, way, c).start()

        c = step - deep

        @pl.when(jnp.logical_and(c >= 0, c < chunks))
        def _():
            @pl.when(p == 0)
            def _():
                block_onward(block_in, c)

            @pl.when(p > 0)
            def _():
                block_copy(block_in, 0, c).wait_recv()
                block_onward(block_out, c)

    @pl.loop(0, chunks)
    def _(c):
        for way in range(2):
            @pl.when(ways[way][0] < ncol - 1)
            def _(way=way):
                column_copy(column_in, way, c).wait_send()

            @pl.when(targets[way][1])
            def _(way=way):
                block_copy(block_in, way, c).wait_send()

    for way in range(2):
        @pl.when(targets[way][1])
        def _(way=way):
            lead_copy(lead_in, way).wait_send()
    for d in range(1, ncol):
        peer_copy(lead_in, d).wait_send()
        peer_copy(lead_in, d).wait_recv()


CHUNKS = 8


def spread(column, block, lead, ncol, nrow):
    dma = pltpu.SemaphoreType.DMA
    anywhere = pl.BlockSpec(memory_space=pl.ANY)
    sent = 4 * 2 * (column.size + block.size)
    return pl.pallas_call(
        functools.partial(spread_kernel, ncol, nrow, CHUNKS),
        in_specs=[anywhere] * 3,
        out_specs=[anywhere] * 3,
        out_shape=[
            jax.ShapeDtypeStruct(column.shape, F32),
            jax.ShapeDtypeStruct(block.shape, F32),
            jax.ShapeDtypeStruct((ncol,) + lead.shape, F32),
        ],
        scratch_shapes=[
            dma((2, CHUNKS)), dma((2, CHUNKS)), dma((2, CHUNKS)), dma((CHUNKS,)),
            dma((2,)), dma, dma((ncol,)), dma((ncol,)), dma,
        ],
        cost_estimate=pl.CostEstimate(flops=0, bytes_accessed=20 * sent, transcendentals=0),
        compiler_params=pltpu.CompilerParams(
            collective_id=0, has_side_effects=True, vmem_limit_bytes=8 * 2**20
        ),
    )(column, block, lead)


def shards(normal, panel_inverse, rhs, shifts):
    high = lax.Precision.HIGHEST
    row_index = lax.axis_index("row")
    col_index = lax.axis_index("col")
    nrow = lax.axis_size("row")
    ncol = lax.axis_size("col")
    spacing = ncol // nrow
    brows, nb, bcols = (normal.shape[0], normal.shape[2], normal.shape[3])
    narrow = rhs.shape[3]
    wide = narrow * ncol
    right = jnp.transpose(rhs[:, 0], (0, 2, 1))
    gathered = lax.all_gather(right, "col", axis=0)
    column_in = normal[:, 0, :, 0, 0, :].reshape(brows * nb, nb)
    block_in = normal[0, 0].reshape(nb, bcols * nb)
    column, across, leading = spread(column_in, block_in, right[0], ncol, nrow)
    column = jnp.where(col_index == 0, column_in, column)
    across = jnp.where(row_index == 0, block_in, across)
    panel = jnp.dot(column, panel_inverse.T, precision=high, preferred_element_type=F32)
    across = jnp.dot(panel_inverse, across, precision=high, preferred_element_type=F32)
    first = jnp.dot(
        leading.reshape(wide, nb), panel_inverse.T, precision=high,
        preferred_element_type=F32,
    )
    tile = normal.reshape(brows * nb * bcols * nb // LANES, LANES)
    schur, reduced, total = fused(
        tile, panel, across, gathered, first, brows, bcols, nb, narrow
    )
    part = lax.psum_scatter(total, "row", scatter_dimension=0, tiled=True)
    part = part.reshape(spacing, narrow, bcols * nb)
    offset = col_index // nrow
    arrived = []
    for t in range(spacing):
        moves = [
            (p * ncol + q, (q % nrow) * ncol + spacing * p + (q // nrow + t) % spacing)
            for p in range(nrow)
            for q in range(ncol)
        ]
        piece = lax.dynamic_index_in_dim(part, (offset + t) % spacing, 0, keepdims=False)
        arrived.append(lax.ppermute(piece, ("row", "col"), moves))
    arrived = jnp.stack(arrived)
    place = col_index % spacing
    ordered = [
        lax.dynamic_index_in_dim(arrived, (place - o + spacing) % spacing, 0, keepdims=False)
        for o in range(spacing)
    ]
    product = jnp.stack([o.reshape(narrow, bcols, nb) for o in ordered])
    product = jnp.transpose(product, (2, 0, 1, 3)).reshape(brows, narrow, nb)
    scales = lax.dynamic_slice_in_dim(jnp.repeat(shifts, R), col_index * narrow, narrow)
    applied = product + reduced * scales[None, :, None]
    back = lambda value: jnp.transpose(value, (0, 2, 1)).reshape(brows, 1, nb, narrow)
    return (schur.reshape(normal.shape), back(reduced), back(applied))


def solution(mesh):
    in_specs = (P(None, "row", None, None, "col", None), P(), P(None, "row", None, "col"), P())
    out_specs = (
        P(None, "row", None, None, "col", None),
        P(None, "row", None, "col"),
        P(None, "row", None, "col"),
    )
    return jax.shard_map(shards, mesh=mesh, in_specs=in_specs, out_specs=out_specs, check_vma=False)
```

```python
import functools

import jax
import jax.numpy as jnp
from jax import lax
from jax.experimental import pallas as pl
from jax.experimental.pallas import tpu as pltpu
from jax.sharding import PartitionSpec as P

R = 128
LANES = 128
F32 = jnp.float32
BF16 = jnp.bfloat16


def split(value):
    high = value.astype(BF16)
    low = (value - high.astype(F32)).astype(BF16)
    return high, low


def left_of(value):
    high, low = split(value)
    return jnp.concatenate([high, high, low], axis=1)


def right_of(value):
    high, low = split(value)
    return jnp.concatenate([high, low, high], axis=0)


def dot(left, right):
    return jnp.dot(left, right, preferred_element_type=F32)


def fused_kernel(bcols, nb, narrow, tile_ref, panel_ref, across_ref, rhs_ref, first_ref,
                 schur_ref, own_ref, rest_ref, total_ref, across3, first3, reduced):
    step = pl.program_id(0)
    stride = bcols * nb // LANES
    per = nb // LANES
    wide = first_ref.shape[0]

    @pl.when(step == 0)
    def _():
        across3[...] = right_of(across_ref[...])
        first3[...] = left_of(first_ref[...])
        total_ref[...] = jnp.zeros_like(total_ref)

    panel = panel_ref[...]
    panel3 = left_of(panel)
    high, low = split(panel)
    flat3 = jnp.concatenate([high, low, high], axis=1)
    lowered = lax.dot_general(
        first3[...], flat3, (((1,), (1,)), ((), ())), preferred_element_type=F32
    )
    value = rhs_ref[...].reshape(wide, nb) - lowered
    leading = jnp.logical_and(step == 0, lax.axis_index("row") == 0)
    value = jnp.where(leading, first_ref[...], value)
    reduced[...] = value
    mine = pl.multiple_of(lax.axis_index("col") * narrow, narrow)
    own_ref[0] = reduced[pl.ds(mine, narrow), :]
    nrow = lax.axis_size("row")
    spacing = lax.axis_size("col") // nrow
    offset = lax.axis_index("col") // nrow
    groups = []
    for t in range(spacing):
        which = (offset + t) % spacing
        groups.append(jnp.concatenate([
            reduced[pl.ds(pl.multiple_of((p * spacing + which) * narrow, narrow), narrow), :]
            for p in range(nrow)
        ], axis=0))
    for t in range(1, spacing):
        rest_ref[t - 1, 0] = groups[t]
    value3 = left_of(groups[0])
    for b in range(bcols):
        columns = slice(b * nb, (b + 1) * nb)
        product = dot(panel3, across3[:, columns])
        parts = []
        for h in range(per):
            rows = pl.ds(b * per + h, nb, stride=stride)
            part = tile_ref[rows, :] - product[:, h * LANES:(h + 1) * LANES]
            schur_ref[rows, :] = part
            parts.append(part)
        updated = jnp.concatenate(parts, axis=1)
        total_ref[:, columns] += dot(value3, right_of(updated))


def fused(tile, panel, across, gathered, first, brows, bcols, nb, narrow):
    wide = first.shape[0]
    ncol = wide // narrow
    chunk = nb * bcols * nb // LANES
    spacing = ncol // lax.axis_size("row")
    group = wide // spacing
    rest = max(spacing - 1, 1)
    whole = lambda i: (0, 0)
    return pl.pallas_call(
        functools.partial(fused_kernel, bcols, nb, narrow),
        grid=(brows,),
        in_specs=[
            pl.BlockSpec((chunk, LANES), lambda i: (i, 0)),
            pl.BlockSpec((nb, nb), lambda i: (i, 0)),
            pl.BlockSpec((nb, bcols * nb), whole),
            pl.BlockSpec((ncol, None, narrow, nb), lambda i: (0, i, 0, 0)),
            pl.BlockSpec((wide, nb), whole),
        ],
        out_specs=[
            pl.BlockSpec((chunk, LANES), lambda i: (i, 0)),
            pl.BlockSpec((1, narrow, nb), lambda i: (i, 0, 0)),
            pl.BlockSpec((rest, 1, group, nb), lambda i: (0, i, 0, 0)),
            pl.BlockSpec((group, bcols * nb), whole),
        ],
        out_shape=[
            jax.ShapeDtypeStruct(tile.shape, F32),
            jax.ShapeDtypeStruct((brows, narrow, nb), F32),
            jax.ShapeDtypeStruct((rest, brows, group, nb), F32),
            jax.ShapeDtypeStruct((group, bcols * nb), F32),
        ],
        scratch_shapes=[
            pltpu.VMEM((3 * nb, bcols * nb), BF16),
            pltpu.VMEM((wide, 3 * nb), BF16),
            pltpu.VMEM((wide, nb), F32),
        ],
        compiler_params=pltpu.CompilerParams(
            dimension_semantics=("arbitrary",), vmem_limit_bytes=48 * 2**20
        ),
    )(tile, panel, across, gathered, first)


def later_kernel(bcols, nb, schur_ref, value_ref, total_ref):
    stride = bcols * nb // LANES
    per = nb // LANES

    @pl.when(pl.program_id(0) == 0)
    def _():
        total_ref[...] = jnp.zeros_like(total_ref)

    value3 = left_of(value_ref[...])
    for b in range(bcols):
        updated = jnp.concatenate([
            schur_ref[pl.ds(b * per + h, nb, stride=stride), :] for h in range(per)
        ], axis=1)
        total_ref[:, b * nb:(b + 1) * nb] += dot(value3, right_of(updated))


def later(schur, values, index, bcols, nb):
    brows, group = values.shape[1:3]
    chunk = nb * bcols * nb // LANES
    return pl.pallas_call(
        functools.partial(later_kernel, bcols, nb),
        grid=(brows,),
        in_specs=[
            pl.BlockSpec((chunk, LANES), lambda i: (i, 0)),
            pl.BlockSpec((None, None, group, nb), lambda i: (index, i, 0, 0)),
        ],
        out_specs=pl.BlockSpec((group, bcols * nb), lambda i: (0, 0)),
        out_shape=jax.ShapeDtypeStruct((group, bcols * nb), F32),
        cost_estimate=pl.CostEstimate(
            flops=6 * schur.size * group, bytes_accessed=4 * (schur.size + brows * group * nb),
            transcendentals=0,
        ),
        compiler_params=pltpu.CompilerParams(
            dimension_semantics=("arbitrary",), vmem_limit_bytes=32 * 2**20
        ),
    )(schur, values)


def spread_kernel(ncol, nrow, chunks, column_in, block_in, lead_in,
                  column_out, block_out, lead_out,
                  column_send, column_recv, block_send, block_recv,
                  lead_send, lead_recv, peer_send, peer_recv, local):
    p = lax.axis_index("row")
    q = lax.axis_index("col")
    barrier = pltpu.get_barrier_semaphore()
    for d in range(1, ncol):
        pl.semaphore_signal(barrier, inc=1, device_id={"col": (q + d) % ncol})
    for d in range(1, nrow):
        pl.semaphore_signal(barrier, inc=1, device_id={"row": (p + d) % nrow})
    pl.semaphore_wait(barrier, ncol + nrow - 2)

    targets = [(p + 1, jnp.logical_and(p % 2 == 0, p + 1 < nrow)),
               (p + 2, jnp.logical_and(p % 2 == 0, p + 2 < nrow))]

    def lead_copy(source, way):
        return pltpu.make_async_remote_copy(
            source, lead_out.at[q], lead_send.at[way], lead_recv,
            device_id={"row": targets[way][0] % nrow})

    def peer_copy(source, d):
        return pltpu.make_async_remote_copy(
            source, lead_out.at[q], peer_send.at[d], peer_recv.at[d],
            device_id={"col": (q + d) % ncol})

    def lead_onward(source):
        for way in range(2):
            @pl.when(targets[way][1])
            def _(way=way):
                lead_copy(source, way).start()
        for d in range(1, ncol):
            peer_copy(source, d).start()

    @pl.when(p == 0)
    def _():
        pltpu.make_async_copy(lead_in, lead_out.at[q], local).start()
        lead_onward(lead_in)
        pltpu.make_async_copy(lead_in, lead_out.at[q], local).wait()

    @pl.when(p > 0)
    def _():
        lead_copy(lead_in, 0).wait_recv()
        lead_onward(lead_out.at[q])

    odd = q % 2
    place = (1 - odd) * (q // 2) + odd * (ncol - 1 - q // 2)

    def at_place(k):
        k = k % ncol
        late = k // (ncol // 2)
        return (1 - late) * 2 * k + late * (2 * (ncol - 1 - k) + 1)

    ways = [(place, at_place(place + 1)), ((ncol - place) % ncol, at_place(place + ncol - 1))]
    size = column_in.shape[0] // (2 * chunks)
    thin = block_in.shape[0] // chunks

    def column_copy(source, way, c):
        rows = pl.ds(pl.multiple_of((way * chunks + c) * size, size), size)
        return pltpu.make_async_remote_copy(
            source.at[rows], column_out.at[rows], column_send.at[way, c],
            column_recv.at[way, c], device_id={"col": ways[way][1]})

    def block_copy(source, way, c):
        rows = pl.ds(pl.multiple_of(c * thin, thin), thin)
        return pltpu.make_async_remote_copy(
            source.at[rows], block_out.at[rows], block_send.at[way, c],
            block_recv.at[c], device_id={"row": targets[way][0] % nrow})

    def block_onward(source, c):
        for way in range(2):
            @pl.when(targets[way][1])
            def _(way=way):
                block_copy(source, way, c).start()

    deep = p // 2 + p % 2

    @pl.loop(0, chunks + ncol + nrow)
    def _(step):
        for way in range(2):
            depth = ways[way][0]
            c = step - depth

            @pl.when(jnp.logical_and(c >= 0, c < chunks))
            def _(way=way, depth=depth, c=c):
                @pl.when(depth == 0)
                def _():
                    column_copy(column_in, way, c).start()

                @pl.when(depth > 0)
                def _():
                    column_copy(column_in, way, c).wait_recv()

                    @pl.when(depth < ncol - 1)
                    def _():
                        column_copy(column_out, way, c).start()

        c = step - deep

        @pl.when(jnp.logical_and(c >= 0, c < chunks))
        def _():
            @pl.when(p == 0)
            def _():
                block_onward(block_in, c)

            @pl.when(p > 0)
            def _():
                block_copy(block_in, 0, c).wait_recv()
                block_onward(block_out, c)

    @pl.loop(0, chunks)
    def _(c):
        for way in range(2):
            @pl.when(ways[way][0] < ncol - 1)
            def _(way=way):
                column_copy(column_in, way, c).wait_send()

            @pl.when(targets[way][1])
            def _(way=way):
                block_copy(block_in, way, c).wait_send()

    for way in range(2):
        @pl.when(targets[way][1])
        def _(way=way):
            lead_copy(lead_in, way).wait_send()
    for d in range(1, ncol):
        peer_copy(lead_in, d).wait_send()
        peer_copy(lead_in, d).wait_recv()


CHUNKS = 8


def spread(column, block, lead, ncol, nrow):
    dma = pltpu.SemaphoreType.DMA
    anywhere = pl.BlockSpec(memory_space=pl.ANY)
    sent = 4 * 2 * (column.size + block.size)
    return pl.pallas_call(
        functools.partial(spread_kernel, ncol, nrow, CHUNKS),
        in_specs=[anywhere] * 3,
        out_specs=[anywhere] * 3,
        out_shape=[
            jax.ShapeDtypeStruct(column.shape, F32),
            jax.ShapeDtypeStruct(block.shape, F32),
            jax.ShapeDtypeStruct((ncol,) + lead.shape, F32),
        ],
        scratch_shapes=[
            dma((2, CHUNKS)), dma((2, CHUNKS)), dma((2, CHUNKS)), dma((CHUNKS,)),
            dma((2,)), dma, dma((ncol,)), dma((ncol,)), dma,
        ],
        cost_estimate=pl.CostEstimate(flops=0, bytes_accessed=20 * sent, transcendentals=0),
        compiler_params=pltpu.CompilerParams(
            collective_id=0, has_side_effects=True, vmem_limit_bytes=8 * 2**20
        ),
    )(column, block, lead)


def shards(normal, panel_inverse, rhs, shifts):
    high = lax.Precision.HIGHEST
    row_index = lax.axis_index("row")
    col_index = lax.axis_index("col")
    nrow = lax.axis_size("row")
    ncol = lax.axis_size("col")
    spacing = ncol // nrow
    brows, nb, bcols = (normal.shape[0], normal.shape[2], normal.shape[3])
    narrow = rhs.shape[3]
    wide = narrow * ncol
    right = jnp.transpose(rhs[:, 0], (0, 2, 1))
    gathered = lax.all_gather(right, "col", axis=0)
    column_in = normal[:, 0, :, 0, 0, :].reshape(brows * nb, nb)
    block_in = normal[0, 0].reshape(nb, bcols * nb)
    column, across, leading = spread(column_in, block_in, right[0], ncol, nrow)
    column = jnp.where(col_index == 0, column_in, column)
    across = jnp.where(row_index == 0, block_in, across)
    panel = jnp.dot(column, panel_inverse.T, precision=high, preferred_element_type=F32)
    across = jnp.dot(panel_inverse, across, precision=high, preferred_element_type=F32)
    first = jnp.dot(
        leading.reshape(wide, nb), panel_inverse.T, precision=high,
        preferred_element_type=F32,
    )
    tile = normal.reshape(brows * nb * bcols * nb // LANES, LANES)
    schur, reduced, values, total = fused(
        tile, panel, across, gathered, first, brows, bcols, nb, narrow
    )
    arrived = []
    for t in range(spacing):
        moves = [
            (p * ncol + q, (q % nrow) * ncol + spacing * p + (q // nrow + t) % spacing)
            for p in range(nrow)
            for q in range(ncol)
        ]
        if t > 0:
            total = later(schur, values, t - 1, bcols, nb)
        piece = lax.psum_scatter(total, "row", scatter_dimension=0, tiled=True)
        arrived.append(lax.ppermute(piece, ("row", "col"), moves))
    arrived = jnp.stack(arrived)
    place = col_index % spacing
    ordered = [
        lax.dynamic_index_in_dim(arrived, (place - o + spacing) % spacing, 0, keepdims=False)
        for o in range(spacing)
    ]
    product = jnp.stack([o.reshape(narrow, bcols, nb) for o in ordered])
    product = jnp.transpose(product, (2, 0, 1, 3)).reshape(brows, narrow, nb)
    scales = lax.dynamic_slice_in_dim(jnp.repeat(shifts, R), col_index * narrow, narrow)
    applied = product + reduced * scales[None, :, None]
    back = lambda value: jnp.transpose(value, (0, 2, 1)).reshape(brows, 1, nb, narrow)
    return (schur.reshape(normal.shape), back(reduced), back(applied))


def solution(mesh):
    in_specs = (P(None, "row", None, None, "col", None), P(), P(None, "row", None, "col"), P())
    out_specs = (
        P(None, "row", None, None, "col", None),
        P(None, "row", None, "col"),
        P(None, "row", None, "col"),
    )
    return jax.shard_map(shards, mesh=mesh, in_specs=in_specs, out_specs=out_specs, check_vma=False)
```
